32 devices in a mesh: grp: 2 (over y), seq: 4 (over z), head: 2 (over x), rep: 2 (over core).
Axes of the slice: x: 2, y: 2, z: 4, core: 2. Of those that a mesh axis runs over, the one named last changes fastest.
Arguments:
- light_qkv: bfloat16 [8192, 3, 512], P(('grp', 'seq'), None, ('head', 'rep')), parts along dimension 0, may hold values from -40 to 40
- heavy_qkv: bfloat16 [1024, 3, 512], P(('grp', 'seq'), None, ('head', 'rep')), parts along dimension 0, may hold values from -40 to 40
- grad_out: bfloat16 [8192, 512], P(('grp', 'seq'), ('head', 'rep')), parts along dimension 0, may hold values from -6 to 6
- blocks: int32 [16], P(('grp', 'seq')), parts along dimension 0, may hold values from 0 to 15, as said below
- counts: int32 [8], P(('grp', 'seq')), parts along dimension 0, may hold values from 1 to 2, as said below
Outputs:
- attended: bfloat16 [8192, 512], P(('grp', 'seq'), ('head', 'rep')), parts along dimension 0
- grad_light: bfloat16 [8192, 3, 512], P(('grp', 'seq'), None, ('head', 'rep')), parts along dimension 0
- grad_heavy: bfloat16 [1024, 3, 512], P(('grp', 'seq'), None, ('head', 'rep')), parts along dimension 0
The draws below stay inside these ranges and needn't reach their ends.
There are 2 independent parts, one for each index of `grp`. The reference program is written for one: setup_inputs(seed, part) draws one part's arguments, and reference() takes and returns one part's arrays. A program takes and returns all parts, laid end to end along the dimension named above; each array names one. Nothing has to cross between parts.
Inputs may be any that keep to these rules, and one draw needn't show every extreme that they name: `blocks`: the 2 entries of one shard are distinct. `counts`: some shard routes 2 blocks and some shard routes 1.
All inputs are finite; a program needn't handle non-finite values.
Results may differ from the reference program's by a relative error of at most 0.0081.
Values may be sent and summed in bfloat16 or wider, within the bound.
No kernel may reach another device: no remote copies, remote signals or barrier semaphores. Data moves between devices by JAX's collectives and lax.ppermute only.
A program may use at most 64 MiB of HBM per device.

```python
import jax
import jax.numpy as jnp
from jax import lax

HEAD_DIM = 64
WIN = 128
BLK = 64
CAP = 2
TOK_DEV = 1024
HEADS = 8
TOKENS = 4096
SLOTS = 512


def attention_draw(key, row_total):
    subkeys = jax.random.split(key, 1)
    features = HEADS * HEAD_DIM
    drawn = jnp.clip(jax.random.normal(subkeys[0], (row_total, 3, features), jnp.float32), -6.0, 6.0)
    q_tilt = jnp.array([2.5, 1.0, 1.0], jnp.float32).reshape(1, 3, 1)
    return (drawn * q_tilt).astype(jnp.bfloat16)


def draw_light_qkv(key, part):
    return attention_draw(jax.random.fold_in(key, 3), TOKENS)


def draw_heavy_qkv(key, part):
    return attention_draw(jax.random.fold_in(key, 7), SLOTS)


def draw_counts(key, part):
    shards = TOKENS // TOK_DEV
    key_one, key_two, key_three, key_four = jax.random.split(jax.random.fold_in(key, 11), 4)
    first_draw = jax.random.randint(key_one, (shards,), 0, 4)
    second = jax.random.randint(key_two, (shards,), 0, 4)
    routed = 1 + first_draw * second * (CAP - 1) // 9
    busiest = jax.random.randint(key_three, (), 0, shards)
    lightest = (busiest + 1 + jax.random.randint(key_four, (), 0, shards - 1)) % shards
    position = jnp.arange(shards)
    routed = jnp.where(position == busiest, CAP, routed)
    routed = jnp.where(position == lightest, 1, routed)
    return jnp.minimum(routed, CAP).astype(jnp.int32)


def draw_blocks(key, part):
    shards = TOKENS // TOK_DEV
    per_shard = TOK_DEV // BLK
    key_one, key_two, key_three = jax.random.split(jax.random.fold_in(key, 13), 3)
    raw_attention_table = jax.random.randint(key_one, (shards, per_shard), 0, 1 << 20) * per_shard + jnp.arange(per_shard)[None, :]
    top_shard = jax.random.randint(key_two, (), 0, shards)
    low_shard = (top_shard + 1 + jax.random.randint(key_three, (), 0, shards - 1)) % shards
    rows_at = jnp.arange(shards)[:, None]
    column = jnp.arange(per_shard)[None, :]
    raw_attention_table = jnp.where((rows_at == top_shard) & (column == per_shard - 1), -1, raw_attention_table)
    raw_attention_table = jnp.where((rows_at == low_shard) & (column == 0), -1, raw_attention_table)
    block_order = jnp.argsort(raw_attention_table, axis=1)[:, :CAP]
    return block_order.reshape(shards * CAP).astype(jnp.int32)


def level_of(own_key, dims, cuts, least, high):
    factor_of, own = 1.0, jax.random.fold_in(own_key, 6)
    for axis_at, shards_of in cuts:
        heights = jnp.exp(jax.random.uniform(jax.random.fold_in(own, axis_at), (shards_of,), jnp.float32, least / len(cuts), high / len(cuts)))
        factor_of = factor_of * jnp.repeat(heights, dims[axis_at] // shards_of).reshape([-1 if axis == axis_at else 1 for axis in range(len(dims))])
    return factor_of


def gaussian(rng, extent, scale, reach, cuts=(), held_as=jnp.bfloat16):
    values = scale * jax.random.normal(rng, extent, jnp.float32)
    if cuts:
        values = values * level_of(rng, extent, cuts, -0.22, 0.18)
    return jnp.clip(values, -reach, reach).astype(held_as)


def setup_inputs(seed: int = 0, part: int = 0) -> dict:
    seeds = jax.random.split(jax.random.key(seed), 6)
    own_keys = jax.random.split(jax.random.fold_in(seeds[5], part), 6)
    light_qkv = draw_light_qkv(jax.random.fold_in(jax.random.fold_in(seeds[5], part), 71), part)
    heavy_qkv = draw_heavy_qkv(jax.random.fold_in(jax.random.fold_in(seeds[5], part), 71), part)
    grad_out = gaussian(own_keys[2], (TOKENS, HEADS * HEAD_DIM), 1.0, 6.0, ((0, 4), (1, 4)))
    blocks = draw_blocks(jax.random.fold_in(jax.random.fold_in(seeds[5], part), 71), part)
    counts = draw_counts(jax.random.fold_in(jax.random.fold_in(seeds[5], part), 71), part)
    return {"light_qkv": light_qkv, "heavy_qkv": heavy_qkv, "grad_out": grad_out, "blocks": blocks, "counts": counts}


def window_stack(values, block_count):
    pieces = values.reshape((block_count + 2, WIN) + values.shape[1:])
    return jnp.concatenate([pieces[:-2], pieces[1:-1], pieces[2:]], axis=1)


def window_fold(terms_in, block_count):
    pieces = terms_in.reshape((block_count, 3, WIN) + terms_in.shape[2:])
    pad_tail = [(0, 0)] * (terms_in.ndim - 1)
    folded = jnp.pad(pieces[:, 0], [(0, 2)] + pad_tail) + jnp.pad(pieces[:, 1], [(1, 1)] + pad_tail) + jnp.pad(pieces[:, 2], [(2, 0)] + pad_tail)
    return folded.reshape(((block_count + 2) * WIN,) + terms_in.shape[2:])


def band_mask(first_row, block_count, total_rows):
    q_pos = jnp.arange(WIN)[None, :, None]
    k_pos = jnp.arange(3 * WIN)[None, None, :]
    block_at = jnp.arange(block_count)[:, None, None]
    global_key = first_row + (block_at - 1) * WIN + k_pos
    return (k_pos >= q_pos) & (k_pos <= q_pos + 2 * WIN) & (global_key >= 0) & (global_key < total_rows)


def masked_softmax(raw_attention_table, inside):
    masked = jnp.where(inside, raw_attention_table, -jnp.inf)
    row_top = jnp.max(masked, axis=-1, keepdims=True)
    log_total = row_top + jnp.log(jnp.sum(jnp.exp(masked - row_top), axis=-1, keepdims=True))
    return log_total[..., 0], jnp.exp(masked - log_total)


def light_head(operands):
    queries, keys_in, values_in, dout_head = operands
    block_count = TOKENS // WIN
    inverse_root_factor = HEAD_DIM ** -0.5
    rim_pad = [(WIN, WIN), (0, 0)]
    neighbour_lookups = window_stack(jnp.pad(keys_in, rim_pad), block_count).astype(jnp.float32)
    neighbour_contents = window_stack(jnp.pad(values_in, rim_pad), block_count).astype(jnp.float32)
    question_tiles = queries.reshape(block_count, WIN, HEAD_DIM).astype(jnp.float32)
    cotangent_tiles = dout_head.reshape(block_count, WIN, HEAD_DIM).astype(jnp.float32)
    inside = band_mask(0, block_count, TOKENS)
    raw_attention_table = jnp.einsum("elu,egu->elg", question_tiles, neighbour_lookups) * inverse_root_factor
    light_lse, light_probs = masked_softmax(raw_attention_table, inside)
    weight_matrix = lax.optimization_barrier(light_probs.astype(jnp.bfloat16)).astype(jnp.float32)
    light_output = jnp.einsum("lrm,lmz->lrz", weight_matrix, neighbour_contents)
    light_delta = jnp.sum(cotangent_tiles * light_output, axis=-1)
    softmax_cotangent = jnp.einsum("elu,egu->elg", cotangent_tiles, neighbour_contents)
    score_gradient = lax.optimization_barrier((light_probs * (softmax_cotangent - light_delta[..., None])).astype(jnp.bfloat16)).astype(jnp.float32)
    light_query_gradient = jnp.einsum("lrm,lmz->lrz", score_gradient, neighbour_lookups) * inverse_root_factor
    key_window_gradient = jnp.einsum("xfi,xfc->xic", score_gradient, question_tiles) * inverse_root_factor
    value_window_gradient = jnp.einsum("xfi,xfc->xic", weight_matrix, cotangent_tiles)
    light_dk = window_fold(key_window_gradient, block_count)[WIN:WIN + TOKENS]
    light_dv = window_fold(value_window_gradient, block_count)[WIN:WIN + TOKENS]
    return light_output.reshape(TOKENS, HEAD_DIM), light_query_gradient.reshape(TOKENS, HEAD_DIM), light_dk, light_dv


def heavy_head(operands, live_slot):
    queries, keys_in, values_in, dout_head = operands
    inverse_root_factor = HEAD_DIM ** -0.5
    raw_attention_table = jnp.dot(queries, keys_in.T, preferred_element_type=jnp.float32) * inverse_root_factor
    heavy_lse, heavy_probs = masked_softmax(raw_attention_table, live_slot[None, :])
    weight_matrix = heavy_probs.astype(jnp.bfloat16)
    heavy_out = jnp.where(live_slot[:, None], jnp.dot(weight_matrix, values_in, preferred_element_type=jnp.float32), 0.0)
    heavy_delta = jnp.sum(dout_head.astype(jnp.float32) * heavy_out, axis=-1)
    softmax_cotangent = jnp.dot(dout_head, values_in.T, preferred_element_type=jnp.float32)
    score_gradient = (heavy_probs * (softmax_cotangent - heavy_delta[:, None])).astype(jnp.bfloat16)
    heavy_dq = jnp.dot(score_gradient, keys_in, preferred_element_type=jnp.float32) * inverse_root_factor
    heavy_dk = jnp.dot(score_gradient.T, queries, preferred_element_type=jnp.float32) * inverse_root_factor
    heavy_dv = jnp.dot(weight_matrix.T, dout_head, preferred_element_type=jnp.float32)
    return heavy_out, heavy_dq, heavy_dk, heavy_dv


def merge_heads(stacked_heads):
    return stacked_heads.transpose(1, 0, 2).reshape(stacked_heads.shape[1], -1)


def reference(light_qkv, heavy_qkv, grad_out, blocks, counts):
    features = light_qkv.shape[2]
    head_count = features // HEAD_DIM
    slot_total = heavy_qkv.shape[0]
    light_heads = light_qkv.reshape(TOKENS, 3, head_count, HEAD_DIM).transpose(1, 2, 0, 3)
    dout_heads = grad_out.reshape(TOKENS, head_count, HEAD_DIM).transpose(1, 0, 2)
    light_parts = lax.map(light_head, (light_heads[0], light_heads[1], light_heads[2], dout_heads))
    slot_index = jnp.arange(slot_total, dtype=jnp.int32)
    shard_of = slot_index // (CAP * BLK)
    block_of = (slot_index // BLK) % CAP
    live_slot = block_of < counts[shard_of]
    heavy_rows = (shard_of * TOK_DEV + blocks[shard_of * CAP + block_of] * BLK + slot_index % BLK).astype(jnp.int32)
    heavy_dout = jnp.where(live_slot[:, None], grad_out[heavy_rows], jnp.zeros((), grad_out.dtype))
    heavy_heads = heavy_qkv.reshape(slot_total, 3, head_count, HEAD_DIM).transpose(1, 2, 0, 3)
    hdout_heads = heavy_dout.reshape(slot_total, head_count, HEAD_DIM).transpose(1, 0, 2)
    heavy_parts = lax.map(lambda operands: heavy_head(operands, live_slot), (heavy_heads[0], heavy_heads[1], heavy_heads[2], hdout_heads))
    light_output = merge_heads(light_parts[0])
    heavy_out = merge_heads(heavy_parts[0])
    attended = light_output.at[heavy_rows].add(heavy_out).astype(jnp.bfloat16)
    grad_light = jnp.stack([merge_heads(light_parts[position]) for position in (1, 2, 3)], 1).astype(jnp.bfloat16)
    grad_heavy = jnp.stack([merge_heads(heavy_parts[position]) for position in (1, 2, 3)], 1).astype(jnp.bfloat16)
    return attended, grad_light, grad_heavy
```

```python
import functools

import jax
import jax.numpy as jnp
from jax import lax
from jax.experimental import pallas as pl
from jax.experimental.pallas import tpu as pltpu
from jax.sharding import PartitionSpec as P

HEAD_DIM = 64
WIN = 128
BLK = 64
CAP = 2
FEAT = 2 * HEAD_DIM
SLOT = CAP * BLK
FLAGS = 16
HEAVY = 4 * SLOT + FLAGS
HALO = 6 * WIN
SCALE = HEAD_DIM**-0.5

F32 = jnp.float32
BF16 = jnp.bfloat16
SMEM = pl.BlockSpec(memory_space=pltpu.SMEM)
VMEM = pl.BlockSpec(memory_space=pltpu.VMEM)
ANY = pl.BlockSpec(memory_space=pl.ANY)


def dot_nt(left, right):
    return lax.dot_general(left, right, (((1,), (1,)), ((), ())), preferred_element_type=F32)


def dot_nn(left, right):
    return jnp.dot(left, right, preferred_element_type=F32)


def by_head(rows):
    low = lax.broadcasted_iota(jnp.int32, rows.shape, 1) < HEAD_DIM
    zero = jnp.zeros_like(rows)
    return jnp.concatenate([jnp.where(low, rows, zero), jnp.where(low, zero, rows)], axis=0)


def own_head(columns):
    n = columns.shape[1] // 2
    return jnp.concatenate([columns[:HEAD_DIM, :n], columns[HEAD_DIM:, n:]], axis=0)


def triangles():
    key = lax.broadcasted_iota(jnp.int32, (WIN, 2 * WIN), 0)
    query = lax.broadcasted_iota(jnp.int32, (WIN, 2 * WIN), 1) % WIN
    return key >= query, key <= query


def probabilities(scores):
    top = jnp.max(scores, axis=0, keepdims=True)
    raised = jnp.exp(scores - top)
    return raised * (1.0 / jnp.sum(raised, axis=0, keepdims=True))


def deltas(cot_t, out_t):
    terms = cot_t * out_t
    return jnp.concatenate(
        [
            jnp.sum(terms[:HEAD_DIM], axis=0, keepdims=True),
            jnp.sum(terms[HEAD_DIM:], axis=0, keepdims=True),
        ],
        axis=1,
    )


def band(scores, low, high):
    return jnp.concatenate(
        [
            jnp.where(low, scores[:WIN], -jnp.inf),
            scores[WIN : 2 * WIN],
            jnp.where(high, scores[2 * WIN :], -jnp.inf),
        ],
        axis=0,
    )


def light_block(queries, cot, keys, values, values_t, low, high):
    q_pair = by_head(queries * jnp.asarray(SCALE, BF16))
    d_pair = by_head(cot)
    probs = probabilities(band(dot_nt(keys, q_pair), low, high))
    weights = probs.astype(BF16)
    out_t = own_head(dot_nn(values_t, weights))
    delta = deltas(cot.T.astype(F32), out_t)
    dscores = (probs * (dot_nt(values, d_pair) - delta)).astype(BF16)
    return weights, dscores, out_t, q_pair, d_pair


def pack_kernel(blocks, counts, heavy, light, grad_out, right, left, middle, copied, sems):
    rows = light.shape[1]
    copies = []
    for place, edge, one in ((right, rows - 2 * WIN, rows - WIN), (left, 0, 0)):
        for source, target, count in (
            (light.at[1, pl.ds(edge, 2 * WIN)], HEAVY, 2 * WIN),
            (light.at[2, pl.ds(edge, 2 * WIN)], HEAVY + 2 * WIN, 2 * WIN),
            (light.at[0, pl.ds(one, WIN)], HEAVY + 4 * WIN, WIN),
            (grad_out.at[pl.ds(one, WIN)], HEAVY + 5 * WIN, WIN),
        ):
            copies.append(
                pltpu.make_async_copy(
                    source, place.at[pl.ds(target, count)], sems.at[len(copies)]
                )
            )
    slot_copies = []
    for block_at in range(CAP):
        start = pl.multiple_of(blocks[block_at] * BLK, BLK)
        slot_copies.append(
            pltpu.make_async_copy(
                grad_out.at[pl.ds(start, BLK)],
                copied.at[pl.ds(block_at * BLK, BLK)],
                sems.at[len(copies) + block_at],
            )
        )
    for copy in slot_copies + copies:
        copy.start()
    flags = [
        jnp.full((FLAGS // CAP, FEAT), (block_at < counts[0]).astype(F32))
        for block_at in range(CAP)
    ]
    flags = jnp.concatenate(flags, axis=0).astype(BF16)
    for place in (right, left, middle):
        for at, part in enumerate((1, 2, 0)):
            place[at * SLOT : (at + 1) * SLOT] = heavy[part]
        place[4 * SLOT : HEAVY] = flags
    for copy in slot_copies:
        copy.wait()
    for block_at in range(CAP):
        piece = copied[block_at * BLK : (block_at + 1) * BLK]
        piece = jnp.where(block_at < counts[0], piece, jnp.zeros_like(piece))
        for place in (right, left, middle):
            place[3 * SLOT + block_at * BLK : 3 * SLOT + (block_at + 1) * BLK] = piece
    for copy in copies:
        copy.wait()


def inner_kernel(light, grad_out, out, grads, rim, keys_t, values_t, sums):
    block_count = light.shape[1] // WIN
    low, high = triangles()
    for at in range(block_count):
        span = slice(at * WIN, (at + 1) * WIN)
        keys_t[:, span] = light[1, span].T
        values_t[:, span] = light[2, span].T
    touched = set()
    for at in range(1, block_count - 1):
        span = slice(at * WIN, (at + 1) * WIN)
        window = slice((at - 1) * WIN, (at + 2) * WIN)
        weights, dscores, out_t, q_pair, d_pair = light_block(
            light[0, span],
            grad_out[span],
            light[1, window],
            light[2, window],
            values_t[:, window],
            low,
            high,
        )
        out[span] = out_t.T
        dq_t = own_head(dot_nn(keys_t[:, window], dscores)) * SCALE
        grads[0, span] = dq_t.T.astype(BF16)
        dk = dot_nn(dscores, q_pair)
        dv = dot_nn(weights, d_pair)
        for place in range(3):
            target = at - 1 + place
            rows = slice(target * WIN, (target + 1) * WIN)
            part = slice(place * WIN, (place + 1) * WIN)
            for which, term in ((0, dk[part]), (1, dv[part])):
                if target in touched:
                    term = sums[which, rows] + term
                sums[which, rows] = term
            touched.add(target)
    edge = 2 * WIN
    last = (block_count - 2) * WIN
    for which in range(2):
        grads[1 + which, edge:last] = sums[which, edge:last].astype(BF16)
        rim[which, :edge] = sums[which, :edge]
        rim[which, edge:] = sums[which, last:]


def outer_kernel(
    ranks,
    blocks,
    counts,
    own_right,
    own_left,
    from_left,
    from_right,
    from_middle,
    out,
    rim,
    grads_in,
    attended,
    grads,
    grad_heavy,
    combined,
    dq_stage,
    kv_stage,
    k_all,
    v_all,
    q_all,
    d_all,
    sems,
):
    rows = out.shape[0]
    edge = 2 * WIN
    low, high = triangles()
    inner = slice(WIN, rows - WIN)
    combined[inner] = out[inner]
    has_left = ranks[0] > 0
    has_right = ranks[0] < ranks[1] - 1
    copies = []

    def halo(ref, part, count):
        starts = (HEAVY, HEAVY + edge, HEAVY + 2 * edge, HEAVY + 2 * edge + WIN)
        return ref[starts[part] : starts[part] + count]

    for side in range(2):
        if side == 0:
            first, second, exists = from_left, own_left, has_left
        else:
            first, second, exists = own_right, from_right, has_right
        keys = jnp.concatenate([halo(first, 0, edge), halo(second, 0, edge)], axis=0)
        values = jnp.concatenate([halo(first, 1, edge), halo(second, 1, edge)], axis=0)
        keys_t, values_t = keys.T, values.T
        total = []
        for which in range(2):
            total.append(rim[which, side * edge : (side + 1) * edge])
        for place, ref in ((0, first), (1, second)):
            window = slice(place * WIN, (place + 3) * WIN)
            own = place == 1 - side
            below, above = low, high
            if own and side == 0:
                below = low & exists
            if own and side == 1:
                above = high & exists
            weights, dscores, out_t, q_pair, d_pair = light_block(
                halo(ref, 2, WIN),
                halo(ref, 3, WIN),
                keys[window],
                values[window],
                values_t[:, window],
                below,
                above,
            )
            if own:
                span = slice(0, WIN) if side == 0 else slice(rows - WIN, rows)
                combined[span] = out_t.T
                dq_t = own_head(dot_nn(keys_t[:, window], dscores)) * SCALE
                dq_stage[side] = dq_t.T.astype(BF16)
                part = slice(WIN, 3 * WIN) if side == 0 else slice(0, 2 * WIN)
            else:
                part = slice(2 * WIN, 3 * WIN) if side == 0 else slice(0, WIN)
            for which, left, right in ((0, dscores[part], q_pair), (1, weights[part], d_pair)):
                term = dot_nn(left, right)
                if not own:
                    term = jnp.where(exists, term, 0.0)
                    pad = jnp.zeros_like(term)
                    term = jnp.concatenate([term, pad] if side == 0 else [pad, term], axis=0)
                total[which] = total[which] + term
        place = 0 if side == 0 else rows - edge
        for which in range(2):
            kv_stage[which, side] = total[which].astype(BF16)
            copies.append(
                pltpu.make_async_copy(
                    kv_stage.at[which, side],
                    grads.at[1 + which, pl.ds(place, edge)],
                    sems.at[3 * side + which],
                )
            )
        place = 0 if side == 0 else rows - WIN
        copies.append(
            pltpu.make_async_copy(
                dq_stage.at[side], grads.at[0, pl.ds(place, WIN)], sems.at[3 * side + 2]
            )
        )
        for copy in copies[-3:]:
            copy.start()

    pieces = [(own_right, 0), (from_left, 0)]
    pieces += [(from_middle, at * HEAVY) for at in range(from_middle.shape[0] // HEAVY)]
    pieces += [(from_right, 0)]
    live = []
    for at, (ref, base) in enumerate(pieces):
        span = slice(at * SLOT, (at + 1) * SLOT)
        k_all[span] = ref[base : base + SLOT]
        v_all[span] = ref[base + SLOT : base + 2 * SLOT]
        q_all[span] = ref[base + 2 * SLOT : base + 3 * SLOT] * jnp.asarray(SCALE, BF16)
        d_all[span] = ref[base + 3 * SLOT : base + 4 * SLOT]
        flags = ref[base + 4 * SLOT : base + HEAVY].astype(F32)
        for block_at in range(CAP):
            row = block_at * FLAGS // CAP
            flag = flags[row : row + 1]
            live.append(jnp.concatenate([flag, flag], axis=1) > 0)
    keys, values = k_all[...], v_all[...]
    values_t = values.T

    def heavy_chunk(at):
        start = at * SLOT
        if not isinstance(at, int):
            start = pl.multiple_of(start, SLOT)
        queries, cot = q_all[pl.ds(start, SLOT)], d_all[pl.ds(start, SLOT)]
        q_pair, d_pair = by_head(queries), by_head(cot)
        scores = dot_nt(keys, q_pair)
        scores = jnp.concatenate(
            [
                jnp.where(flag, scores[slot * BLK : (slot + 1) * BLK], -jnp.inf)
                for slot, flag in enumerate(live)
            ],
            axis=0,
        )
        probs = probabilities(scores)
        weights = probs.astype(BF16)
        out_t = own_head(dot_nn(values_t, weights))
        delta = deltas(cot.T.astype(F32), out_t)
        own = isinstance(at, int) and at == 0
        reach = keys.shape[0] if own else SLOT
        dprobs = dot_nt(values[:reach], d_pair)
        dscores = (probs[:reach] * (dprobs - delta)).astype(BF16)
        dk = dot_nn(dscores[:SLOT], q_pair)
        dv = dot_nn(weights[:SLOT], d_pair)
        return dk, dv, out_t, dscores

    dk, dv, out_t, dscores = heavy_chunk(0)
    dq_t = own_head(dot_nn(keys.T, dscores)) * SCALE
    grad_heavy[0] = dq_t.T.astype(BF16)
    heavy_out = out_t.T

    def more(at, sums):
        terms = heavy_chunk(at)
        return sums[0] + terms[0], sums[1] + terms[1]

    if len(pieces) <= 4:
        for at in range(1, len(pieces)):
            dk, dv = more(at, (dk, dv))
    else:
        dk, dv = lax.fori_loop(1, len(pieces), more, (dk, dv))
    grad_heavy[1] = dk.astype(BF16)
    grad_heavy[2] = dv.astype(BF16)
    for block_at in range(CAP):
        start = pl.multiple_of(blocks[block_at] * BLK, BLK)
        term = heavy_out[block_at * BLK : (block_at + 1) * BLK]
        term = jnp.where(block_at < counts[0], term, 0.0)
        combined[pl.ds(start, BLK)] = combined[pl.ds(start, BLK)] + term
    attended[...] = combined[...].astype(BF16)
    for copy in copies:
        copy.wait()


def local(seq_size, light_qkv, heavy_qkv, grad_out, blocks, counts):
    rows, features = grad_out.shape
    slots = heavy_qkv.shape[0]
    assert features == FEAT and slots == SLOT and seq_size >= 4
    block_count = rows // WIN
    light = jnp.transpose(light_qkv, (1, 0, 2))
    heavy = jnp.transpose(heavy_qkv, (1, 0, 2))
    side = jax.ShapeDtypeStruct((HEAVY + HALO, FEAT), BF16)
    right, left, middle = pl.pallas_call(
        pack_kernel,
        name="pack",
        out_shape=(side, side, jax.ShapeDtypeStruct((HEAVY, FEAT), BF16)),
        in_specs=[SMEM, SMEM, VMEM, ANY, ANY],
        out_specs=[VMEM] * 3,
        scratch_shapes=[pltpu.VMEM((SLOT, FEAT), BF16), pltpu.SemaphoreType.DMA((8 + CAP,))],
    )(blocks, counts, heavy, light, grad_out)

    def shifted(value, step):
        return lax.ppermute(
            value, "seq", [(at, (at + step) % seq_size) for at in range(seq_size)]
        )

    from_left = shifted(right, 1)
    from_right = shifted(left, seq_size - 1)
    middles = [shifted(middle, step) for step in range(2, seq_size - 1)]
    from_middle = middles[0] if len(middles) == 1 else jnp.concatenate(middles, axis=0)

    matmuls = 2 * 6 * 3 * WIN * 2 * WIN * FEAT
    out, grads, rim = pl.pallas_call(
        inner_kernel,
        name="inner",
        out_shape=(
            jax.ShapeDtypeStruct((rows, FEAT), F32),
            jax.ShapeDtypeStruct((3, rows, FEAT), BF16),
            jax.ShapeDtypeStruct((2, 4 * WIN, FEAT), F32),
        ),
        in_specs=[VMEM, VMEM],
        out_specs=[VMEM] * 3,
        scratch_shapes=[
            pltpu.VMEM((FEAT, rows), BF16),
            pltpu.VMEM((FEAT, rows), BF16),
            pltpu.VMEM((2, rows, FEAT), F32),
        ],
        cost_estimate=pl.CostEstimate(
            flops=(block_count - 2) * matmuls * 8,
            bytes_accessed=rows * FEAT * 20,
            transcendentals=(block_count - 2) * 3 * WIN * 2 * WIN,
        ),
    )(light, grad_out)

    ranks = jnp.stack([lax.axis_index("seq"), jnp.int32(seq_size)]).astype(jnp.int32)
    all_slots = SLOT * seq_size
    attended, grads, grad_heavy = pl.pallas_call(
        outer_kernel,
        name="outer",
        out_shape=(
            jax.ShapeDtypeStruct((rows, FEAT), BF16),
            jax.ShapeDtypeStruct((3, rows, FEAT), BF16),
            jax.ShapeDtypeStruct((3, SLOT, FEAT), BF16),
        ),
        in_specs=[SMEM] * 3 + [VMEM] * 7 + [ANY],
        out_specs=[VMEM, ANY, VMEM],
        scratch_shapes=[
            pltpu.VMEM((rows, FEAT), F32),
            pltpu.VMEM((2, WIN, FEAT), BF16),
            pltpu.VMEM((2, 2, 2 * WIN, FEAT), BF16),
            pltpu.VMEM((all_slots, FEAT), BF16),
            pltpu.VMEM((all_slots, FEAT), BF16),
            pltpu.VMEM((all_slots, FEAT), BF16),
            pltpu.VMEM((all_slots, FEAT), BF16),
            pltpu.SemaphoreType.DMA((6,)),
        ],
        input_output_aliases={10: 1},
    )(ranks, blocks, counts, right, left, from_left, from_right, from_middle, out, rim, grads)
    return (
        attended,
        jnp.transpose(grads, (1, 0, 2)),
        jnp.transpose(grad_heavy, (1, 0, 2)),
    )


def solution(mesh):
    flat = P(("grp", "seq"), ("head", "rep"))
    deep = P(("grp", "seq"), None, ("head", "rep"))
    line = P(("grp", "seq"))
    return jax.shard_map(
        functools.partial(local, mesh.shape["seq"]),
        mesh=mesh,
        in_specs=(deep, deep, flat, line, line),
        out_specs=(flat, deep, deep),
        check_vma=False,
    )
```

```python
import functools

import jax
import jax.numpy as jnp
from jax import lax
from jax.experimental import pallas as pl
from jax.experimental.pallas import tpu as pltpu
from jax.sharding import PartitionSpec as P


HEAD_DIM = 64
WIN = 128
BLK = 64
CAP = 2
FEAT = 2 * HEAD_DIM
SLOT = CAP * BLK
FLAGS = 16
HEAVY = 4 * SLOT + FLAGS
HALO = 6 * WIN
SCALE = HEAD_DIM**-0.5

F32 = jnp.float32
BF16 = jnp.bfloat16
SMEM = pl.BlockSpec(memory_space=pltpu.SMEM)
VMEM = pl.BlockSpec(memory_space=pltpu.VMEM)
ANY = pl.BlockSpec(memory_space=pl.ANY)


def limit(mebibytes):
    return pltpu.CompilerParams(vmem_limit_bytes=mebibytes << 20)


def dot_nt(left, right):
    return lax.dot_general(left, right, (((1,), (1,)), ((), ())), preferred_element_type=F32)


def dot_nn(left, right):
    return jnp.dot(left, right, preferred_element_type=F32)


def by_head(rows):
    low = lax.broadcasted_iota(jnp.int32, rows.shape, 1) < HEAD_DIM
    zero = jnp.zeros_like(rows)
    return jnp.concatenate([jnp.where(low, rows, zero), jnp.where(low, zero, rows)], axis=0)


def own_head(columns):
    n = columns.shape[1] // 2
    return jnp.concatenate([columns[:HEAD_DIM, :n], columns[HEAD_DIM:, n:]], axis=0)


def triangles():
    key = lax.broadcasted_iota(jnp.int32, (WIN, 2 * WIN), 0)
    query = lax.broadcasted_iota(jnp.int32, (WIN, 2 * WIN), 1) % WIN
    return key >= query, key <= query


def probabilities(scores):
    top = jnp.max(scores, axis=0, keepdims=True)
    raised = jnp.exp(scores - top)
    return raised * (1.0 / jnp.sum(raised, axis=0, keepdims=True))


def deltas(cot_t, out_t):
    terms = cot_t * out_t
    return jnp.concatenate(
        [
            jnp.sum(terms[:HEAD_DIM], axis=0, keepdims=True),
            jnp.sum(terms[HEAD_DIM:], axis=0, keepdims=True),
        ],
        axis=1,
    )


def band(scores, low, high):
    return jnp.concatenate(
        [
            jnp.where(low, scores[:WIN], -jnp.inf),
            scores[WIN : 2 * WIN],
            jnp.where(high, scores[2 * WIN :], -jnp.inf),
        ],
        axis=0,
    )


def light_block(queries, cot, keys, values, values_t, low, high):
    q_pair = by_head(queries * jnp.asarray(SCALE, BF16))
    d_pair = by_head(cot)
    probs = probabilities(band(dot_nt(keys, q_pair), low, high))
    weights = probs.astype(BF16)
    out_t = own_head(dot_nn(values_t, weights))
    delta = deltas(cot.T.astype(F32), out_t)
    dscores = (probs * (dot_nt(values, d_pair) - delta)).astype(BF16)
    return weights, dscores, out_t, q_pair, d_pair


def pack_kernel(blocks, counts, heavy, light, grad_out, right, left, middle):
    rows = light.shape[1]
    flags = [
        jnp.full((FLAGS // CAP, FEAT), (block_at < counts[0]).astype(F32))
        for block_at in range(CAP)
    ]
    flags = jnp.concatenate(flags, axis=0).astype(BF16)
    cots = []
    for block_at in range(CAP):
        start = pl.multiple_of(blocks[block_at] * BLK, BLK)
        cot = grad_out[pl.ds(start, BLK)]
        cots.append(jnp.where(block_at < counts[0], cot, jnp.zeros_like(cot)))
    for place in (right, left, middle):
        for at, part in enumerate((1, 2, 0)):
            place[at * SLOT : (at + 1) * SLOT] = heavy[part]
        for block_at, cot in enumerate(cots):
            target = 3 * SLOT + block_at * BLK
            place[target : target + BLK] = cot
        place[4 * SLOT : HEAVY] = flags
    for place, edge, one in ((right, rows - 2 * WIN, rows - WIN), (left, 0, 0)):
        place[HEAVY : HEAVY + 2 * WIN] = light[1, edge : edge + 2 * WIN]
        place[HEAVY + 2 * WIN : HEAVY + 4 * WIN] = light[2, edge : edge + 2 * WIN]
        place[HEAVY + 4 * WIN : HEAVY + 5 * WIN] = light[0, one : one + WIN]
        place[HEAVY + 5 * WIN : HEAVY + 6 * WIN] = grad_out[one : one + WIN]


def inner_kernel(light, grad_out, out, grads, rim, keys_t, values_t, sums):
    block_count = light.shape[1] // WIN
    low, high = triangles()
    for at in range(block_count):
        span = slice(at * WIN, (at + 1) * WIN)
        keys_t[:, span] = light[1, span].T
        values_t[:, span] = light[2, span].T
    touched = set()
    for at in range(1, block_count - 1):
        span = slice(at * WIN, (at + 1) * WIN)
        window = slice((at - 1) * WIN, (at + 2) * WIN)
        weights, dscores, out_t, q_pair, d_pair = light_block(
            light[0, span],
            grad_out[span],
            light[1, window],
            light[2, window],
            values_t[:, window],
            low,
            high,
        )
        out[span] = out_t.T
        dq_t = own_head(dot_nn(keys_t[:, window], dscores)) * SCALE
        grads[0, span] = dq_t.T.astype(BF16)
        dk = dot_nn(dscores, q_pair)
        dv = dot_nn(weights, d_pair)
        for place in range(3):
            target = at - 1 + place
            rows = slice(target * WIN, (target + 1) * WIN)
            part = slice(place * WIN, (place + 1) * WIN)
            for which, term in ((0, dk[part]), (1, dv[part])):
                if target in touched:
                    term = sums[which, rows] + term
                sums[which, rows] = term
            touched.add(target)
    edge = 2 * WIN
    last = (block_count - 2) * WIN
    for which in range(2):
        grads[1 + which, edge:last] = sums[which, edge:last].astype(BF16)
        rim[which, :edge] = sums[which, :edge]
        rim[which, edge:] = sums[which, last:]


def edge_kernel(
    blocks,
    own_right,
    own_left,
    from_left,
    from_right,
    out,
    rim,
    grads_in,
    attended,
    routed,
    grads,
    combined,
    dq_stage,
    kv_stage,
    sems,
):
    rows = out.shape[0]
    edge = 2 * WIN
    low, high = triangles()
    inner = slice(WIN, rows - WIN)
    combined[inner] = out[inner]
    position = lax.axis_index("seq")
    has_left = position > 0
    has_right = position < lax.axis_size("seq") - 1
    copies = []

    def halo(ref, part, count):
        starts = (HEAVY, HEAVY + edge, HEAVY + 2 * edge, HEAVY + 2 * edge + WIN)
        return ref[starts[part] : starts[part] + count]

    for side in range(2):
        if side == 0:
            first, second, exists = from_left, own_left, has_left
        else:
            first, second, exists = own_right, from_right, has_right
        keys = jnp.concatenate([halo(first, 0, edge), halo(second, 0, edge)], axis=0)
        values = jnp.concatenate([halo(first, 1, edge), halo(second, 1, edge)], axis=0)
        keys_t, values_t = keys.T, values.T
        total = [rim[which, side * edge : (side + 1) * edge] for which in range(2)]
        for place, ref in ((0, first), (1, second)):
            window = slice(place * WIN, (place + 3) * WIN)
            own = place == 1 - side
            below = low & exists if own and side == 0 else low
            above = high & exists if own and side == 1 else high
            weights, dscores, out_t, q_pair, d_pair = light_block(
                halo(ref, 2, WIN),
                halo(ref, 3, WIN),
                keys[window],
                values[window],
                values_t[:, window],
                below,
                above,
            )
            if own:
                span = slice(0, WIN) if side == 0 else slice(rows - WIN, rows)
                combined[span] = out_t.T
                dq_t = own_head(dot_nn(keys_t[:, window], dscores)) * SCALE
                dq_stage[side] = dq_t.T.astype(BF16)
                part = slice(WIN, 3 * WIN) if side == 0 else slice(0, 2 * WIN)
            else:
                part = slice(2 * WIN, 3 * WIN) if side == 0 else slice(0, WIN)
            for which, left, right in ((0, dscores[part], q_pair), (1, weights[part], d_pair)):
                term = dot_nn(left, right)
                if not own:
                    term = jnp.where(exists, term, 0.0)
                    pad = jnp.zeros_like(term)
                    term = jnp.concatenate([term, pad] if side == 0 else [pad, term], axis=0)
                total[which] = total[which] + term
        place = 0 if side == 0 else rows - edge
        for which in range(2):
            kv_stage[which, side] = total[which].astype(BF16)
            copies.append(
                pltpu.make_async_copy(
                    kv_stage.at[which, side],
                    grads.at[1 + which, pl.ds(place, edge)],
                    sems.at[3 * side + which],
                )
            )
        place = 0 if side == 0 else rows - WIN
        copies.append(
            pltpu.make_async_copy(
                dq_stage.at[side], grads.at[0, pl.ds(place, WIN)], sems.at[3 * side + 2]
            )
        )
        for copy in copies[-3:]:
            copy.start()
    attended[...] = combined[...].astype(BF16)
    for block_at in range(CAP):
        start = pl.multiple_of(blocks[block_at] * BLK, BLK)
        routed[block_at * BLK : (block_at + 1) * BLK] = combined[pl.ds(start, BLK)]
    for copy in copies:
        copy.wait()


def heavy_kernel(
    blocks,
    counts,
    own,
    from_left,
    from_right,
    from_middle,
    from_end,
    routed,
    attended_in,
    attended,
    grad_heavy,
    stage,
    k_all,
    v_all,
    q_all,
    d_all,
    sems,
):
    position = lax.axis_index("seq")
    has_left = position > 0
    has_right = position < lax.axis_size("seq") - 1
    pieces = [(own, 0, None), (from_left, 0, has_left)]
    pieces += [(from_middle, at * HEAVY, None) for at in range(from_middle.shape[0] // HEAVY)]
    pieces += [(from_right, 0, has_right)]
    live = []
    for at, (ref, base, exists) in enumerate(pieces):
        span = slice(at * SLOT, (at + 1) * SLOT)

        def rows(start, count):
            value = ref[base + start : base + start + count]
            if exists is None:
                return value
            return jnp.where(exists, value, from_end[start : start + count])

        k_all[span] = rows(0, SLOT)
        v_all[span] = rows(SLOT, SLOT)
        q_all[span] = rows(2 * SLOT, SLOT) * jnp.asarray(SCALE, BF16)
        d_all[span] = rows(3 * SLOT, SLOT)
        flags = rows(4 * SLOT, FLAGS).astype(F32)
        for block_at in range(CAP):
            row = block_at * FLAGS // CAP
            flag = flags[row : row + 1]
            live.append(jnp.concatenate([flag, flag], axis=1) > 0)
    keys, values = k_all[...], v_all[...]
    values_t = values.T

    def heavy_chunk(at):
        start = at * SLOT
        if not isinstance(at, int):
            start = pl.multiple_of(start, SLOT)
        queries, cot = q_all[pl.ds(start, SLOT)], d_all[pl.ds(start, SLOT)]
        q_pair, d_pair = by_head(queries), by_head(cot)
        scores = dot_nt(keys, q_pair)
        scores = jnp.concatenate(
            [
                jnp.where(flag, scores[slot * BLK : (slot + 1) * BLK], -jnp.inf)
                for slot, flag in enumerate(live)
            ],
            axis=0,
        )
        probs = probabilities(scores)
        weights = probs.astype(BF16)
        out_t = own_head(dot_nn(values_t, weights))
        delta = deltas(cot.T.astype(F32), out_t)
        mine = isinstance(at, int) and at == 0
        reach = keys.shape[0] if mine else SLOT
        dprobs = dot_nt(values[:reach], d_pair)
        dscores = (probs[:reach] * (dprobs - delta)).astype(BF16)
        dk = dot_nn(dscores[:SLOT], q_pair)
        dv = dot_nn(weights[:SLOT], d_pair)
        return dk, dv, out_t, dscores

    dk, dv, out_t, dscores = heavy_chunk(0)
    heavy_out = out_t.T
    copies = []
    for block_at in range(CAP):
        span = slice(block_at * BLK, (block_at + 1) * BLK)
        term = jnp.where(block_at < counts[0], heavy_out[span], 0.0)
        stage[span] = (routed[span] + term).astype(BF16)
        start = pl.multiple_of(blocks[block_at] * BLK, BLK)
        copies.append(
            pltpu.make_async_copy(
                stage.at[pl.ds(block_at * BLK, BLK)],
                attended.at[pl.ds(start, BLK)],
                sems.at[block_at],
            )
        )
        copies[-1].start()
    dq_t = own_head(dot_nn(keys.T, dscores)) * SCALE
    grad_heavy[0] = dq_t.T.astype(BF16)

    def more(at, sums):
        terms = heavy_chunk(at)
        return sums[0] + terms[0], sums[1] + terms[1]

    if len(pieces) <= 4:
        for at in range(1, len(pieces)):
            dk, dv = more(at, (dk, dv))
    else:
        dk, dv = lax.fori_loop(1, len(pieces), more, (dk, dv))
    grad_heavy[1] = dk.astype(BF16)
    grad_heavy[2] = dv.astype(BF16)
    for copy in copies:
        copy.wait()


def local(seq_size, light_qkv, heavy_qkv, grad_out, blocks, counts):
    rows, features = grad_out.shape
    slots = heavy_qkv.shape[0]
    assert features == FEAT and slots == SLOT and seq_size >= 4
    block_count = rows // WIN
    light = jnp.transpose(light_qkv, (1, 0, 2))
    heavy = jnp.transpose(heavy_qkv, (1, 0, 2))
    side = jax.ShapeDtypeStruct((HEAVY + HALO, FEAT), BF16)
    right, left, middle = pl.pallas_call(
        pack_kernel,
        name="pack",
        out_shape=(side, side, jax.ShapeDtypeStruct((HEAVY, FEAT), BF16)),
        in_specs=[SMEM, SMEM, VMEM, VMEM, VMEM],
        out_specs=[VMEM] * 3,
        compiler_params=limit(4),
    )(blocks, counts, heavy, light, grad_out)

    end = seq_size - 1

    def send(value, pairs):
        return lax.ppermute(value, "seq", pairs)

    from_left = send(right, [(at, at + 1) for at in range(end)])
    from_right = send(left, [(at + 1, at) for at in range(end)])
    middles = [
        send(middle, [(at, (at + step) % seq_size) for at in range(seq_size)])
        for step in range(2, end)
    ]
    from_middle = middles[0] if len(middles) == 1 else jnp.concatenate(middles, axis=0)
    from_end = send(middle, [(0, end), (end, 0)])

    matmuls = 2 * 6 * 3 * WIN * 2 * WIN * FEAT
    out, grads, rim = pl.pallas_call(
        inner_kernel,
        name="inner",
        out_shape=(
            jax.ShapeDtypeStruct((rows, FEAT), F32),
            jax.ShapeDtypeStruct((3, rows, FEAT), BF16),
            jax.ShapeDtypeStruct((2, 4 * WIN, FEAT), F32),
        ),
        in_specs=[VMEM, VMEM],
        out_specs=[VMEM] * 3,
        scratch_shapes=[
            pltpu.VMEM((FEAT, rows), BF16),
            pltpu.VMEM((FEAT, rows), BF16),
            pltpu.VMEM((2, rows, FEAT), F32),
        ],
        cost_estimate=pl.CostEstimate(
            flops=(block_count - 2) * matmuls * 8,
            bytes_accessed=rows * FEAT * 20,
            transcendentals=(block_count - 2) * 3 * WIN * 2 * WIN,
        ),
        compiler_params=limit(10),
    )(light, grad_out)

    attended, routed, grads = pl.pallas_call(
        edge_kernel,
        name="edge",
        out_shape=(
            jax.ShapeDtypeStruct((rows, FEAT), BF16),
            jax.ShapeDtypeStruct((SLOT, FEAT), F32),
            jax.ShapeDtypeStruct((3, rows, FEAT), BF16),
        ),
        in_specs=[SMEM] + [VMEM] * 6 + [ANY],
        out_specs=[VMEM, VMEM, ANY],
        scratch_shapes=[
            pltpu.VMEM((rows, FEAT), F32),
            pltpu.VMEM((2, WIN, FEAT), BF16),
            pltpu.VMEM((2, 2, 2 * WIN, FEAT), BF16),
            pltpu.SemaphoreType.DMA((6,)),
        ],
        input_output_aliases={7: 2},
        cost_estimate=pl.CostEstimate(
            flops=4 * matmuls * 8,
            bytes_accessed=rows * FEAT * 20,
            transcendentals=4 * 3 * WIN * 2 * WIN,
        ),
        compiler_params=limit(10),
    )(blocks, right, left, from_left, from_right, out, rim, grads)

    all_slots = SLOT * seq_size
    attended, grad_heavy = pl.pallas_call(
        heavy_kernel,
        name="heavy",
        out_shape=(
            jax.ShapeDtypeStruct((rows, FEAT), BF16),
            jax.ShapeDtypeStruct((3, SLOT, FEAT), BF16),
        ),
        in_specs=[SMEM] * 2 + [VMEM] * 6 + [ANY],
        out_specs=[ANY, VMEM],
        scratch_shapes=[
            pltpu.VMEM((SLOT, FEAT), BF16),
            pltpu.VMEM((all_slots, FEAT), BF16),
            pltpu.VMEM((all_slots, FEAT), BF16),
            pltpu.VMEM((all_slots, FEAT), BF16),
            pltpu.VMEM((all_slots, FEAT), BF16),
            pltpu.SemaphoreType.DMA((CAP,)),
        ],
        input_output_aliases={8: 0},
        compiler_params=limit(16 if seq_size <= 4 else 40),
    )(blocks, counts, middle, from_left, from_right, from_middle, from_end, routed, attended)
    return (
        attended,
        jnp.transpose(grads, (1, 0, 2)),
        jnp.transpose(grad_heavy, (1, 0, 2)),
    )


def solution(mesh):
    flat = P(("grp", "seq"), ("head", "rep"))
    deep = P(("grp", "seq"), None, ("head", "rep"))
    line = P(("grp", "seq"))
    return jax.shard_map(
        functools.partial(local, mesh.shape["seq"]),
        mesh=mesh,
        in_specs=(deep, deep, flat, line, line),
        out_specs=(flat, deep, deep),
        check_vma=False,
    )
```

```python
import functools

import jax
import jax.numpy as jnp
from jax import lax
from jax.experimental import pallas as pl
from jax.experimental.pallas import tpu as pltpu
from jax.sharding import PartitionSpec as P


HEAD_DIM = 64
WIN = 128
BLK = 64
CAP = 2
FEAT = 2 * HEAD_DIM
SLOT = CAP * BLK
FLAGS = 16
HEAVY = 4 * SLOT + FLAGS
HALO = 6 * WIN
SCALE = HEAD_DIM**-0.5

F32 = jnp.float32
BF16 = jnp.bfloat16
SMEM = pl.BlockSpec(memory_space=pltpu.SMEM)
VMEM = pl.BlockSpec(memory_space=pltpu.VMEM)
ANY = pl.BlockSpec(memory_space=pl.ANY)


def limit(mebibytes):
    return pltpu.CompilerParams(vmem_limit_bytes=mebibytes << 20)


def dot_nt(left, right):
    return lax.dot_general(left, right, (((1,), (1,)), ((), ())), preferred_element_type=F32)


def dot_nn(left, right):
    return jnp.dot(left, right, preferred_element_type=F32)


def by_head(rows):
    low = lax.broadcasted_iota(jnp.int32, rows.shape, 1) < HEAD_DIM
    zero = jnp.zeros_like(rows)
    return jnp.concatenate([jnp.where(low, rows, zero), jnp.where(low, zero, rows)], axis=0)


def own_head(columns):
    n = columns.shape[1] // 2
    return jnp.concatenate([columns[:HEAD_DIM, :n], columns[HEAD_DIM:, n:]], axis=0)


def triangles():
    key = lax.broadcasted_iota(jnp.int32, (WIN, 2 * WIN), 0)
    query = lax.broadcasted_iota(jnp.int32, (WIN, 2 * WIN), 1) % WIN
    return key >= query, key <= query


def probabilities(scores):
    top = jnp.max(scores, axis=0, keepdims=True)
    raised = jnp.exp(scores - top)
    return raised * (1.0 / jnp.sum(raised, axis=0, keepdims=True))


def deltas(cot_t, out_t):
    terms = cot_t * out_t
    return jnp.concatenate(
        [
            jnp.sum(terms[:HEAD_DIM], axis=0, keepdims=True),
            jnp.sum(terms[HEAD_DIM:], axis=0, keepdims=True),
        ],
        axis=1,
    )


def band(scores, low, high):
    return jnp.concatenate(
        [
            jnp.where(low, scores[:WIN], -jnp.inf),
            scores[WIN : 2 * WIN],
            jnp.where(high, scores[2 * WIN :], -jnp.inf),
        ],
        axis=0,
    )


def light_blocks(blocks):
    scale = jnp.asarray(SCALE, BF16)
    q_pairs = [by_head(block[0] * scale) for block in blocks]
    d_pairs = [by_head(block[1]) for block in blocks]
    scores = [dot_nt(block[2], q_pair) for block, q_pair in zip(blocks, q_pairs)]
    dprobs = [dot_nt(block[3][block[7]], d_pair) for block, d_pair in zip(blocks, d_pairs)]
    cots_t = [block[1].T.astype(F32) for block in blocks]
    probs = [
        probabilities(band(score, block[5], block[6])) for block, score in zip(blocks, scores)
    ]
    weights = [prob.astype(BF16) for prob in probs]
    outs_t = [own_head(dot_nn(block[4], weight)) for block, weight in zip(blocks, weights)]
    shifts = [deltas(cot_t, out_t) for cot_t, out_t in zip(cots_t, outs_t)]
    dscores = [
        (prob[block[7]] * (dprob - shift)).astype(BF16)
        for block, prob, dprob, shift in zip(blocks, probs, dprobs, shifts)
    ]
    weights = [weight[block[7]] for block, weight in zip(blocks, weights)]
    return zip(weights, dscores, outs_t, q_pairs, d_pairs)


def pack_kernel(blocks, counts, heavy, light, grad_out, routed, right, left, sems):
    rows = light.shape[1]
    copies = []

    def move(source, target):
        copies.append(pltpu.make_async_copy(source, target, sems.at[len(copies)]))

    for block_at in range(CAP):
        start = pl.multiple_of(blocks[block_at] * BLK, BLK)
        target = 3 * SLOT + block_at * BLK
        move(grad_out.at[pl.ds(start, BLK)], routed.at[pl.ds(target, BLK)])
    for at, part in enumerate((1, 2, 0)):
        move(heavy.at[part], routed.at[pl.ds(at * SLOT, SLOT)])
    for place, edge, one in ((right, rows - 2 * WIN, rows - WIN), (left, 0, 0)):
        move(light.at[1, pl.ds(edge, 2 * WIN)], place.at[pl.ds(0, 2 * WIN)])
        move(light.at[2, pl.ds(edge, 2 * WIN)], place.at[pl.ds(2 * WIN, 2 * WIN)])
        move(light.at[0, pl.ds(one, WIN)], place.at[pl.ds(4 * WIN, WIN)])
        move(grad_out.at[pl.ds(one, WIN)], place.at[pl.ds(5 * WIN, WIN)])
    for copy in copies:
        copy.start()
    flags = [
        jnp.full((FLAGS // CAP, FEAT), (block_at < counts[0]).astype(F32))
        for block_at in range(CAP)
    ]
    routed[4 * SLOT : HEAVY] = jnp.concatenate(flags, axis=0).astype(BF16)
    for copy in copies:
        copy.wait()
    for block_at in range(CAP):

        @pl.when(block_at >= counts[0])
        def _():
            target = 3 * SLOT + block_at * BLK
            routed[target : target + BLK] = jnp.zeros((BLK, FEAT), BF16)


def inner_kernel(light, grad_out, out, grads, rim, keys_t, values_t, sums):
    block_count = light.shape[1] // WIN
    low, high = triangles()
    for at in range(block_count):
        span = slice(at * WIN, (at + 1) * WIN)
        keys_t[:, span] = light[1, span].T
        values_t[:, span] = light[2, span].T
    touched = set()
    order = list(range(1, block_count - 1))
    for group in [order[at : at + 6] for at in range(0, len(order), 6)]:
        blocks = []
        for at in group:
            span = slice(at * WIN, (at + 1) * WIN)
            window = slice((at - 1) * WIN, (at + 2) * WIN)
            blocks.append(
                (
                    light[0, span],
                    grad_out[span],
                    light[1, window],
                    light[2, window],
                    values_t[:, window],
                    low,
                    high,
                    slice(0, 3 * WIN),
                )
            )
        results = list(zip(group, light_blocks(blocks)))
        for at, (weights, dscores, out_t, q_pair, d_pair) in results:
            span = slice(at * WIN, (at + 1) * WIN)
            window = slice((at - 1) * WIN, (at + 2) * WIN)
            out[span] = out_t.T
            dq_t = own_head(dot_nn(keys_t[:, window], dscores)) * SCALE
            grads[0, span] = dq_t.T.astype(BF16)
            dk = dot_nn(dscores, q_pair)
            dv = dot_nn(weights, d_pair)
            for place in range(3):
                target = at - 1 + place
                rows = slice(target * WIN, (target + 1) * WIN)
                part = slice(place * WIN, (place + 1) * WIN)
                for which, term in ((0, dk[part]), (1, dv[part])):
                    if target in touched:
                        term = sums[which, rows] + term
                    sums[which, rows] = term
                touched.add(target)
    edge = 2 * WIN
    last = (block_count - 2) * WIN
    for which in range(2):
        grads[1 + which, edge:last] = sums[which, edge:last].astype(BF16)
        rim[which, :edge] = sums[which, :edge]
        rim[which, edge:] = sums[which, last:]


def edge_kernel(
    blocks,
    own_right,
    own_left,
    from_left,
    from_right,
    out,
    rim,
    grads_in,
    attended,
    routed,
    grads,
    combined,
    dq_stage,
    kv_stage,
    sems,
):
    rows = out.shape[0]
    edge = 2 * WIN
    low, high = triangles()
    inner = slice(WIN, rows - WIN)
    combined[inner] = out[inner]
    position = lax.axis_index("seq")
    has_left = position > 0
    has_right = position < lax.axis_size("seq") - 1
    copies = []

    def halo(ref, part, count):
        starts = (0, edge, 2 * edge, 2 * edge + WIN)
        return ref[starts[part] : starts[part] + count]

    totals = [[rim[which, side * edge : (side + 1) * edge] for which in range(2)] for side in range(2)]
    tasks = []
    for side in range(2):
        if side == 0:
            first, second, exists = from_left, own_left, has_left
        else:
            first, second, exists = own_right, from_right, has_right
        keys = jnp.concatenate([halo(first, 0, edge), halo(second, 0, edge)], axis=0)
        values = jnp.concatenate([halo(first, 1, edge), halo(second, 1, edge)], axis=0)
        keys_t, values_t = keys.T, values.T
        for place, ref in ((0, first), (1, second)):
            window = slice(place * WIN, (place + 3) * WIN)
            own = place == 1 - side
            below = low & exists if own and side == 0 else low
            above = high & exists if own and side == 1 else high
            if own:
                part = slice(0, 3 * WIN)
            else:
                part = slice(2 * WIN, 3 * WIN) if side == 0 else slice(0, WIN)
            block = (
                halo(ref, 2, WIN),
                halo(ref, 3, WIN),
                keys[window],
                values[window],
                values_t[:, window],
                below,
                above,
                part,
            )
            tasks.append((side, own, exists, keys_t[:, window], block))
    results = []
    for at in range(0, len(tasks), 4):
        results += list(light_blocks([task[4] for task in tasks[at : at + 4]]))
    for (side, own, exists, keys_t, _), result in zip(tasks, results):
        weights, dscores, out_t, q_pair, d_pair = result
        if own:
            span = slice(0, WIN) if side == 0 else slice(rows - WIN, rows)
            combined[span] = out_t.T
            dq_t = own_head(dot_nn(keys_t, dscores)) * SCALE
            dq_stage[side] = dq_t.T.astype(BF16)
            part = slice(WIN, 3 * WIN) if side == 0 else slice(0, 2 * WIN)
            weights, dscores = weights[part], dscores[part]
        for which, left, right in ((0, dscores, q_pair), (1, weights, d_pair)):
            term = dot_nn(left, right)
            if not own:
                term = jnp.where(exists, term, 0.0)
                pad = jnp.zeros_like(term)
                term = jnp.concatenate([term, pad] if side == 0 else [pad, term], axis=0)
            totals[side][which] = totals[side][which] + term
    for side, total in enumerate(totals):
        place = 0 if side == 0 else rows - edge
        for which in range(2):
            kv_stage[which, side] = total[which].astype(BF16)
            copies.append(
                pltpu.make_async_copy(
                    kv_stage.at[which, side],
                    grads.at[1 + which, pl.ds(place, edge)],
                    sems.at[3 * side + which],
                )
            )
        place = 0 if side == 0 else rows - WIN
        copies.append(
            pltpu.make_async_copy(
                dq_stage.at[side], grads.at[0, pl.ds(place, WIN)], sems.at[3 * side + 2]
            )
        )
    for copy in copies:
        copy.start()
    attended[...] = combined[...].astype(BF16)
    for block_at in range(CAP):
        start = pl.multiple_of(blocks[block_at] * BLK, BLK)
        routed[block_at * BLK : (block_at + 1) * BLK] = combined[pl.ds(start, BLK)]
    for copy in copies:
        copy.wait()


def heavy_kernel(blocks, counts, *refs):
    pieces, refs = refs[:-10], refs[-10:]
    routed, _, attended, grad_heavy, stage, k_all, v_all, q_all, d_all, sems = refs
    live = []
    for at, ref in enumerate(pieces):
        span = slice(at * SLOT, (at + 1) * SLOT)
        k_all[span] = ref[:SLOT]
        v_all[span] = ref[SLOT : 2 * SLOT]
        q_all[span] = ref[2 * SLOT : 3 * SLOT] * jnp.asarray(SCALE, BF16)
        d_all[span] = ref[3 * SLOT : 4 * SLOT]
        flags = ref[4 * SLOT :].astype(F32)
        for block_at in range(CAP):
            row = block_at * FLAGS // CAP
            flag = flags[row : row + 1]
            live.append(jnp.concatenate([flag, flag], axis=1) > 0)
    keys, values = k_all[...], v_all[...]
    values_t = values.T

    def heavy_chunks(chunks):
        starts = [
            at * SLOT if isinstance(at, int) else pl.multiple_of(at * SLOT, SLOT) for at in chunks
        ]
        q_pairs = [by_head(q_all[pl.ds(start, SLOT)]) for start in starts]
        cots = [d_all[pl.ds(start, SLOT)] for start in starts]
        d_pairs = [by_head(cot) for cot in cots]
        mine = [isinstance(at, int) and at == 0 for at in chunks]
        reach = [keys.shape[0] if own else SLOT for own in mine]
        scores = [dot_nt(keys, q_pair) for q_pair in q_pairs]
        dprobs = [dot_nt(values[:rows], d_pair) for rows, d_pair in zip(reach, d_pairs)]
        cots_t = [cot.T.astype(F32) for cot in cots]
        scores = [
            jnp.concatenate(
                [
                    jnp.where(flag, score[slot * BLK : (slot + 1) * BLK], -jnp.inf)
                    for slot, flag in enumerate(live)
                ],
                axis=0,
            )
            for score in scores
        ]
        probs = [probabilities(score) for score in scores]
        weights = [prob.astype(BF16) for prob in probs]
        outs_t = [own_head(dot_nn(values_t, weight)) for weight in weights]
        shifts = [deltas(cot_t, out_t) for cot_t, out_t in zip(cots_t, outs_t)]
        dscores = [
            (prob[:rows] * (dprob - shift)).astype(BF16)
            for rows, prob, dprob, shift in zip(reach, probs, dprobs, shifts)
        ]
        dk = dot_nn(
            jnp.concatenate([dscore[:SLOT] for dscore in dscores], axis=1),
            jnp.concatenate(q_pairs, axis=0),
        )
        dv = dot_nn(
            jnp.concatenate([weight[:SLOT] for weight in weights], axis=1),
            jnp.concatenate(d_pairs, axis=0),
        )
        return dk, dv, outs_t[0], dscores[0]

    first = list(range(min(len(pieces), 4)))
    dk, dv, out_t, dscores = heavy_chunks(first)
    heavy_out = out_t.T
    copies = []
    for block_at in range(CAP):
        span = slice(block_at * BLK, (block_at + 1) * BLK)
        term = jnp.where(block_at < counts[0], heavy_out[span], 0.0)
        stage[span] = (routed[span] + term).astype(BF16)
        start = pl.multiple_of(blocks[block_at] * BLK, BLK)
        copies.append(
            pltpu.make_async_copy(
                stage.at[pl.ds(block_at * BLK, BLK)],
                attended.at[pl.ds(start, BLK)],
                sems.at[block_at],
            )
        )
        copies[-1].start()
    dq_t = own_head(dot_nn(keys.T, dscores)) * SCALE
    grad_heavy[0] = dq_t.T.astype(BF16)

    def more(at, sums):
        terms = heavy_chunks([at])
        return sums[0] + terms[0], sums[1] + terms[1]

    if len(pieces) > len(first):
        dk, dv = lax.fori_loop(len(first), len(pieces), more, (dk, dv))
    grad_heavy[1] = dk.astype(BF16)
    grad_heavy[2] = dv.astype(BF16)
    for copy in copies:
        copy.wait()


def local(seq_size, light_qkv, heavy_qkv, grad_out, blocks, counts):
    rows, features = grad_out.shape
    slots = heavy_qkv.shape[0]
    assert features == FEAT and slots == SLOT and seq_size >= 4
    block_count = rows // WIN
    light = jnp.transpose(light_qkv, (1, 0, 2))
    heavy = jnp.transpose(heavy_qkv, (1, 0, 2))
    side = jax.ShapeDtypeStruct((HALO, FEAT), BF16)
    own, right, left = pl.pallas_call(
        pack_kernel,
        name="pack",
        out_shape=(jax.ShapeDtypeStruct((HEAVY, FEAT), BF16), side, side),
        in_specs=[SMEM, SMEM, ANY, ANY, ANY],
        out_specs=[VMEM] * 3,
        scratch_shapes=[pltpu.SemaphoreType.DMA((8 + 3 + CAP,))],
        compiler_params=pltpu.CompilerParams(vmem_limit_bytes=66500000),
    )(blocks, counts, heavy, light, grad_out)

    def send(value, pairs):
        return lax.ppermute(value, "seq", pairs)

    from_left = send(right, [(at, at + 1) for at in range(seq_size - 1)])
    from_right = send(left, [(at + 1, at) for at in range(seq_size - 1)])
    others = [
        send(own, [(at, (at + step) % seq_size) for at in range(seq_size)])
        for step in range(1, seq_size)
    ]

    matmuls = 2 * 6 * 3 * WIN * 2 * WIN * FEAT
    out, grads, rim = pl.pallas_call(
        inner_kernel,
        name="inner",
        out_shape=(
            jax.ShapeDtypeStruct((rows, FEAT), F32),
            jax.ShapeDtypeStruct((3, rows, FEAT), BF16),
            jax.ShapeDtypeStruct((2, 4 * WIN, FEAT), F32),
        ),
        in_specs=[VMEM, VMEM],
        out_specs=[VMEM] * 3,
        scratch_shapes=[
            pltpu.VMEM((FEAT, rows), BF16),
            pltpu.VMEM((FEAT, rows), BF16),
            pltpu.VMEM((2, rows, FEAT), F32),
        ],
        cost_estimate=pl.CostEstimate(
            flops=(block_count - 2) * matmuls * 8,
            bytes_accessed=rows * FEAT * 20,
            transcendentals=(block_count - 2) * 3 * WIN * 2 * WIN,
        ),
        compiler_params=limit(10),
    )(light, grad_out)

    attended, routed, grads = pl.pallas_call(
        edge_kernel,
        name="edge",
        out_shape=(
            jax.ShapeDtypeStruct((rows, FEAT), BF16),
            jax.ShapeDtypeStruct((SLOT, FEAT), F32),
            jax.ShapeDtypeStruct((3, rows, FEAT), BF16),
        ),
        in_specs=[SMEM] + [VMEM] * 6 + [ANY],
        out_specs=[VMEM, VMEM, ANY],
        scratch_shapes=[
            pltpu.VMEM((rows, FEAT), F32),
            pltpu.VMEM((2, WIN, FEAT), BF16),
            pltpu.VMEM((2, 2, 2 * WIN, FEAT), BF16),
            pltpu.SemaphoreType.DMA((6,)),
        ],
        input_output_aliases={7: 2},
        cost_estimate=pl.CostEstimate(
            flops=4 * matmuls * 8,
            bytes_accessed=rows * FEAT * 20,
            transcendentals=4 * 3 * WIN * 2 * WIN,
        ),
        compiler_params=limit(10),
    )(blocks, right, left, from_left, from_right, out, rim, grads)

    all_slots = SLOT * seq_size
    attended, grad_heavy = pl.pallas_call(
        heavy_kernel,
        name="heavy",
        out_shape=(
            jax.ShapeDtypeStruct((rows, FEAT), BF16),
            jax.ShapeDtypeStruct((3, SLOT, FEAT), BF16),
        ),
        in_specs=[SMEM] * 2 + [VMEM] * (seq_size + 1) + [ANY],
        out_specs=[ANY, VMEM],
        scratch_shapes=[
            pltpu.VMEM((SLOT, FEAT), BF16),
            pltpu.VMEM((all_slots, FEAT), BF16),
            pltpu.VMEM((all_slots, FEAT), BF16),
            pltpu.VMEM((all_slots, FEAT), BF16),
            pltpu.VMEM((all_slots, FEAT), BF16),
            pltpu.SemaphoreType.DMA((CAP,)),
        ],
        input_output_aliases={seq_size + 3: 0},
        compiler_params=limit(16 if seq_size <= 4 else 40),
    )(blocks, counts, own, *others, routed, attended)
    return (
        attended,
        jnp.transpose(grads, (1, 0, 2)),
        jnp.transpose(grad_heavy, (1, 0, 2)),
    )


def solution(mesh):
    flat = P(("grp", "seq"), ("head", "rep"))
    deep = P(("grp", "seq"), None, ("head", "rep"))
    line = P(("grp", "seq"))
    return jax.shard_map(
        functools.partial(local, mesh.shape["seq"]),
        mesh=mesh,
        in_specs=(deep, deep, flat, line, line),
        out_specs=(flat, deep, deep),
        check_vma=False,
    )
```
